256 devices in a mesh: chain: 64 (over z, x, core), term: 4 (over y).
Axes of the slice: x: 4, y: 4, z: 8, core: 2. Of those that a mesh axis runs over, the one named last changes fastest.
Arguments:
- psi_guess: float32 [64, 8, 128, 128], P('chain'), may hold values from -6 to 6
- transfer_raw: float32 [64, 8, 128, 128], P('chain'), may hold values from -6 to 6
- left_env: float32 [64, 32, 8, 128, 128], P('chain', 'term'), may hold values from -0.75 to 0.75
- right_env: float32 [64, 32, 8, 128, 128], P('chain', 'term'), may hold values from -0.75 to 0.75
- block_sizes: int32 [64, 2, 8], P('chain'), may hold values from 64 to 128
Outputs:
- psi_out: float32 [64, 8, 128, 128], P('chain', 'term')
- energy: float32 [64], P('chain')
The draws below stay inside these ranges and needn't reach their ends.
All inputs are finite; a program needn't handle non-finite values.
Results may differ from the reference program's by a relative error of at most 0.0003.
Values sent between devices are 32-bit elements; how exact they have to be, the bound alone decides.
No kernel may reach another device: no remote copies, remote signals or barrier semaphores. Data moves between devices by JAX's collectives and lax.ppermute only.
A program may use at most 128 MiB of HBM per device.

```python
import math
import jax
import jax.numpy as jnp
from jax import lax

B = 128
SECT = 8
TERMS = 32
ITERS = 4
NSEG = 64


def draw_block_sizes(key, part):
    values = jax.random.randint(key, (NSEG, 2, SECT), B // 2, B + 1)
    return values.at[:, :, 0].set(B).astype(jnp.int32)


def shard_levels(stream_key, extent, shards, low, largest):
    loudness, own = 1.0, jax.random.fold_in(stream_key, 6)
    for dim, shards_of in shards:
        draws = jnp.exp(jax.random.uniform(jax.random.fold_in(own, dim), (shards_of,), jnp.float32, low / len(shards), largest / len(shards)))
        loudness = loudness * jnp.repeat(draws, extent[dim] // shards_of).reshape([-1 if axis == dim else 1 for axis in range(len(extent))])
    return loudness


def gaussian(own_key, shape, spread, limit, shards=(), kind=jnp.bfloat16):
    result = spread * jax.random.normal(own_key, shape, jnp.float32)
    if shards:
        result = result * shard_levels(own_key, shape, shards, -0.22, 0.18)
    return jnp.clip(result, -limit, limit).astype(kind)


def setup_inputs(seed: int = 0) -> dict:
    streams_of = jax.random.split(jax.random.key(seed), 6)
    return {
        "psi_guess": gaussian(streams_of[0], (NSEG, SECT, B, B), 1.0, 6.0, ((0, 64),), jnp.float32),
        "transfer_raw": gaussian(streams_of[1], (NSEG, SECT, B, B), 1.0, 6.0, ((0, 64),), jnp.float32),
        "left_env": gaussian(streams_of[2], (NSEG, TERMS, SECT, B, B), (0.6 / B ** 0.5), 0.75, ((0, 64), (1, 4)), jnp.float32),
        "right_env": gaussian(streams_of[3], (NSEG, TERMS, SECT, B, B), (0.6 / B ** 0.5), 0.75, ((0, 64), (1, 4)), jnp.float32),
        "block_sizes": draw_block_sizes(jax.random.fold_in(streams_of[5], 71), 0),
    }


precise = lax.Precision.HIGHEST
twist_scale = 0.22
shrink = 1.047
epsilon = 1e-06

def transfer(raw_normal):
    block_len = raw_normal.shape[-1]
    identity = jnp.eye(block_len, dtype=jnp.float32)
    skewed = (raw_normal - jnp.swapaxes(raw_normal, -1, -2)) * (twist_scale / math.sqrt(2.0 * block_len))
    return (identity + skewed) / shrink

def symmetric(raw_normal):
    return 0.5 * (raw_normal + jnp.swapaxes(raw_normal, -1, -2))

def sector_mask(sizes_pair, block_len):
    positions = jnp.arange(block_len, dtype=jnp.int32)
    row_live = (positions[None, :] < sizes_pair[0][:, None]).astype(jnp.float32)
    col_live = (positions[None, :] < sizes_pair[1][:, None]).astype(jnp.float32)
    return row_live[:, :, None] * col_live[:, None, :]

def solve_segment(guess, prefix, suffix, left_raw, right_raw, sizes_pair):
    live_mask = sector_mask(sizes_pair, guess.shape[-1])
    volume = float(guess.size)
    partway = jnp.einsum('tkjl,klm->tkjm', symmetric(left_raw), prefix, precision=precise)
    left_full = jnp.einsum('kji,tkjm->tkim', prefix, partway, precision=precise)
    partway = jnp.einsum('kij,tkjl->tkil', suffix, symmetric(right_raw), precision=precise)
    right_full = jnp.einsum('tkil,kml->tkim', partway, suffix, precision=precise)

    def apply_ham(vector):
        halfway = jnp.einsum('tkij,kjl->tkil', left_full, vector, precision=precise)
        return live_mask * jnp.einsum('tkil,tklm->kim', halfway, right_full, precision=precise)

    def mean_dot(first_arr, second_arr):
        return jnp.sum(first_arr * second_arr) / volume
    started = live_mask * guess
    vector = started / jnp.sqrt(mean_dot(started, started) + epsilon)
    image = apply_ham(vector)
    energy = mean_dot(vector, image)
    for step_index in range(ITERS):
        residual = image - energy * vector
        res_norm = jnp.sqrt(mean_dot(residual, residual) + epsilon)
        along = mean_dot(residual, image) / res_norm
        unit_dir = residual / res_norm
        image_unit = apply_ham(unit_dir)
        curve = mean_dot(unit_dir, image_unit)
        gap_half = 0.5 * (curve - energy)
        lowest = 0.5 * (curve + energy) - jnp.sqrt(gap_half * gap_half + along * along)
        coef_a = along
        coef_b = lowest - energy
        combined = jnp.sqrt(coef_a * coef_a + coef_b * coef_b)
        vector = (coef_a * vector + coef_b * unit_dir) / combined
        image = (coef_a * image + coef_b * image_unit) / combined
        energy = lowest
    return (vector, energy)

def reference(psi_guess, transfer_raw, left_env, right_env, block_sizes):
    identity = jnp.eye(B, dtype=jnp.float32)

    def one_segment(seg_index):
        before = jnp.maximum(seg_index - 1, 0).astype(jnp.int32)
        after = jnp.minimum(seg_index + 1, NSEG - 1).astype(jnp.int32)
        is_first = seg_index == 0
        is_last = seg_index == NSEG - 1
        prefix = jnp.where(is_first, identity[None], transfer(transfer_raw[before]))
        suffix = jnp.where(is_last, identity[None], transfer(transfer_raw[after]))
        return solve_segment(psi_guess[seg_index], prefix, suffix, left_env[before], right_env[after], block_sizes[seg_index])
    vectors, energies = lax.map(one_segment, jnp.arange(NSEG, dtype=jnp.int32))
    return (vectors, energies)
```

```python
import functools
import math

import jax
import jax.numpy as jnp
from jax import lax
from jax.experimental import pallas as pl
from jax.experimental.pallas import tpu as pltpu
from jax.sharding import PartitionSpec as P

ITERS = 4
NVEC = ITERS + 2
twist_scale = 0.22
shrink = 1.047
epsilon = 1e-06

B = 128
HALF = 64
F32 = jnp.float32
BF16 = jnp.bfloat16

OWNED = 2
LOCAL_TERMS = 8
MATS = OWNED * LOCAL_TERMS
DIAG_ROW = MATS * HALF
MSG_ROWS = DIAG_ROW + MATS // 2


def split(value):
    high = value.astype(BF16)
    low = (value - high.astype(F32)).astype(BF16)
    return high, low


def dot(left, right):
    return jnp.dot(left, right, preferred_element_type=F32)


def iotas(rows):
    row = lax.broadcasted_iota(jnp.int32, (rows, B), 0)
    lane = lax.broadcasted_iota(jnp.int32, (rows, B), 1)
    return row, lane


def swap_halves(value):
    return pltpu.roll(value, HALF, 1)


def dress_kernel(segments, place_ref, left_ref, right_ref, raw_ref, alpha_ref, beta_ref):
    step = pl.program_id(0)
    seg = place_ref[0]
    odd = lax.rem(seg, 2) == 1
    edge = jnp.logical_or(seg == 0, seg == segments - 1)
    alpha_left = jnp.logical_xor(odd, edge)
    beta_left = jnp.logical_not(odd)

    raw = raw_ref[0, 0]
    skew = (raw - raw.T) * (twist_scale / math.sqrt(2.0 * B) / shrink)
    row, lane = iotas(B)
    eye = jnp.where(row == lane, 1.0, 0.0).astype(F32)
    sign = jnp.where(odd, 1.0, -1.0).astype(F32)
    diag_a = jnp.where(edge, 1.0, 1.0 / shrink).astype(F32)
    skew_a = jnp.where(edge, 0.0, sign).astype(F32)

    def factors(diag, coef):
        even, odd_part = eye * diag, skew * coef
        high, low = split((even + odd_part) * 0.5)
        right_op = jnp.concatenate([jnp.concatenate([high, low], 1)] * 2, 0)
        high, low = split(even - odd_part)
        left_op = jnp.concatenate([jnp.concatenate([high] * 2, 1), jnp.concatenate([low] * 2, 1)], 0)
        return left_op, right_op

    row_h, lane_h = iotas(HALF)
    keep_top = jnp.logical_or(lane_h >= HALF, lane_h >= row_h)
    on_diag_high = lane_h - HALF == row_h
    on_diag_low = lane_h == row_h

    for take_left, ops, out_ref in (
        (alpha_left, factors(diag_a, skew_a), alpha_ref),
        (beta_left, factors(F32(1.0 / shrink), -sign), beta_ref),
    ):
        left_op, right_op = ops
        for pair in range(2):
            rows = []
            for j in range(2):
                term = 2 * pair + j
                env = jnp.where(take_left, left_ref[0, term, 0], right_ref[0, term, 0])
                high, low = split(env + env.T)
                rows.append(jnp.concatenate([high, low], 1))
            part = dot(jnp.concatenate(rows, 0), right_op)
            high, low = split(part[:, :B] + part[:, B:])
            right_side = jnp.concatenate(
                [jnp.concatenate([high[:B], high[B:]], 1), jnp.concatenate([low[:B], low[B:]], 1)], 0
            )
            full = dot(left_op, right_side)
            full = full[:B] + full[B:]
            diag = jnp.zeros((HALF, B), F32)
            for j in range(2):
                mat = full[:, j * B : (j + 1) * B]
                top, bottom = mat[:HALF], mat[HALF:]
                turned = swap_halves(bottom)
                start = pl.multiple_of((step * 4 + 2 * pair + j) * HALF, HALF)
                out_ref[pl.ds(start, HALF), :] = jnp.where(keep_top, top, turned)
                if j == 0:
                    diag = jnp.where(on_diag_high, bottom, diag)
                else:
                    diag = jnp.where(on_diag_low, turned, diag)
            out_ref[pl.ds(DIAG_ROW + step * 2 + pair, 1), :] = jnp.sum(diag, axis=0, keepdims=True)


def dress(place, left_env, right_env, raw, offset, segments, groups):
    def env_map(step, place):
        sector = OWNED * lax.rem(place[1] + offset, groups) + step // 2
        return (0, lax.rem(step, 2), sector, 0, 0)

    def raw_map(step, place):
        return (0, OWNED * lax.rem(place[1] + offset, groups) + step // 2, 0, 0)

    out = jax.ShapeDtypeStruct((MSG_ROWS, B), F32)
    whole = pl.BlockSpec((MSG_ROWS, B), lambda step, place: (0, 0))
    return pl.pallas_call(
        functools.partial(dress_kernel, segments),
        out_shape=(out, out),
        grid_spec=pltpu.PrefetchScalarGridSpec(
            num_scalar_prefetch=1,
            grid=(4,),
            in_specs=[
                pl.BlockSpec((1, 4, 1, B, B), env_map),
                pl.BlockSpec((1, 4, 1, B, B), env_map),
                pl.BlockSpec((1, 1, B, B), raw_map),
            ],
            out_specs=(whole, whole),
        ),
        compiler_params=pltpu.CompilerParams(
            dimension_semantics=("arbitrary",), vmem_limit_bytes=24 << 20
        ),
        cost_estimate=pl.CostEstimate(flops=32 * 4 * 2 * B**3 * 2, bytes_accessed=5 << 20, transcendentals=0),
        name="dress",
    )(place, left_env, right_env, raw)


def total(value):
    tiles = jnp.sum(value.reshape(OWNED * B // 8, 8, B), axis=0)
    return jnp.sum(jnp.sum(tiles, axis=0, keepdims=True), axis=1, keepdims=True)


def unpack_into(msg_ref, dest_ref, group_index):
    row_h, lane_h = iotas(HALF)
    keep_top = jnp.logical_or(lane_h >= HALF, lane_h >= row_h)
    keep_bottom = jnp.logical_and(lane_h >= HALF, lane_h - HALF < row_h)
    on_diag = lane_h - HALF == row_h

    def body(pair, carry):
        diag_row = msg_ref[pl.ds(DIAG_ROW + pair, 1), :]
        for j in range(2):
            mat = 2 * pair + j
            packed = msg_ref[pl.ds(pl.multiple_of(mat * HALF, HALF), HALF), :]
            turned = swap_halves(packed)
            flipped = jnp.concatenate([packed, turned], 0).T
            diag = diag_row if j == 0 else swap_halves(diag_row)
            top = jnp.where(keep_top, packed, flipped[:HALF])
            bottom = jnp.where(keep_bottom, turned, flipped[HALF:])
            bottom = jnp.where(on_diag, jnp.broadcast_to(diag, (HALF, B)), bottom)
            high, low = split(jnp.concatenate([top, bottom], 0))
            owned, term = mat // LOCAL_TERMS, lax.rem(mat, LOCAL_TERMS)
            start = (owned * 4 * LOCAL_TERMS + group_index * LOCAL_TERMS + term) * B
            dest_ref[pl.ds(pl.multiple_of(start, B), B), :] = jnp.concatenate([high, low], 1)
        return carry

    lax.fori_loop(0, MATS // 2, body, 0)


def krylov_kernel(place_ref, sizes_ref, psi_ref, *refs):
    alphas, betas = refs[0:4], refs[4:8]
    basis_ref, report_ref = refs[8:10]
    left_ref, right_ref, vec_ref, acc_ref, mask_ref = refs[10:]
    odd = lax.rem(place_ref[0], 2) == 1
    group = place_ref[1]
    for d in range(4):
        unpack_into(alphas[d], left_ref, d)
        unpack_into(betas[d], right_ref, d)

    row, lane = iotas(B)
    starts = []
    for owned in range(OWNED):
        rows_live = sizes_ref[0, 0, OWNED * group + owned]
        cols_live = sizes_ref[0, 1, OWNED * group + owned]
        first = jnp.where(odd, cols_live, rows_live)
        second = jnp.where(odd, rows_live, cols_live)
        live = jnp.logical_and(row < first, lane < second)
        mask_ref[owned] = jnp.where(live, 1.0, 0.0).astype(F32)
        guess = psi_ref[0, owned]
        starts.append(jnp.where(odd, guess.T, guess))
    vector = jnp.stack(starts, 0) * mask_ref[...]

    pairs = 4 * LOCAL_TERMS // 2
    span = pairs * 2 * B

    def apply_ham():
        acc_ref[...] = jnp.zeros_like(acc_ref)

        def body(chunk, carry):
            for owned in range(OWNED):
                parts = []
                for sub in range(2):
                    start = owned * span + (chunk * 2 + sub) * 2 * B
                    start = pl.multiple_of(start, 2 * B)
                    half = dot(left_ref[pl.ds(start, 2 * B), :], vec_ref[owned])
                    high, low = split(half[:, :B] + half[:, B:])
                    mid = jnp.concatenate(
                        [jnp.concatenate([high[:B], high[B:]], 1), jnp.concatenate([low[:B], low[B:]], 1)], 0
                    )
                    out = dot(mid, right_ref[pl.ds(start, 2 * B), :])
                    parts.append((out[:B, :B] + out[:B, B:]) + (out[B:, :B] + out[B:, B:]))
                acc_ref[owned] += parts[0] + parts[1]
            return carry

        lax.fori_loop(0, pairs // 2, body, 0)
        return acc_ref[...] * mask_ref[...]

    def inverse_norm(square):
        return jnp.where(square > 0.0, lax.rsqrt(jnp.where(square > 0.0, square, 1.0)), 0.0)

    lane_1 = lax.broadcasted_iota(jnp.int32, (1, B), 1)
    report = jnp.zeros((1, B), F32)
    slot = 0

    def put(report, slot, value):
        return jnp.where(lane_1 == slot, value, report)

    grams = []
    square = total(vector * vector)
    scale = inverse_norm(square)
    report = put(report, 0, square * scale)
    basis_ref[0] = vector * scale
    previous_beta = None
    for step in range(NVEC - 1):
        current = basis_ref[step]
        for owned in range(OWNED):
            high, low = split(current[owned])
            vec_ref[owned] = jnp.concatenate([jnp.concatenate([high, low], 1)] * 2, 0)
        image = apply_ham()
        alpha = total(current * image)
        rest = image - alpha * current
        if step:
            rest = rest - previous_beta * basis_ref[step - 1]
        square = total(rest * rest)
        scale = inverse_norm(square)
        beta = square * scale
        basis_ref[step + 1] = rest * scale
        report = put(report, 1 + step, alpha)
        report = put(report, 1 + (NVEC - 1) + step, beta)
        previous_beta = beta
    slot = 1 + 2 * (NVEC - 1)
    for i in range(NVEC):
        for j in range(i, NVEC):
            report = put(report, slot, total(basis_ref[i] * basis_ref[j]))
            slot += 1
    row_8, _ = iotas(8)
    report_ref[...] = jnp.where(row_8 == group, jnp.broadcast_to(report, (8, B)), 0.0)


def krylov(place, sizes, psi, alphas, betas):
    message = pl.BlockSpec((MSG_ROWS, B), lambda i, place: (0, 0))
    return pl.pallas_call(
        krylov_kernel,
        out_shape=(
            jax.ShapeDtypeStruct((NVEC, OWNED, B, B), F32),
            jax.ShapeDtypeStruct((8, B), F32),
        ),
        grid_spec=pltpu.PrefetchScalarGridSpec(
            num_scalar_prefetch=1,
            grid=(1,),
            in_specs=[
                pl.BlockSpec(memory_space=pltpu.SMEM),
                pl.BlockSpec((1, OWNED, B, B), lambda i, place: (0, place[1], 0, 0)),
            ]
            + [message] * 8,
            out_specs=(
                pl.BlockSpec((NVEC, OWNED, B, B), lambda i, place: (0, 0, 0, 0)),
                pl.BlockSpec((8, B), lambda i, place: (0, 0)),
            ),
            scratch_shapes=[
                pltpu.VMEM((OWNED * 4 * LOCAL_TERMS * B, 2 * B), BF16),
                pltpu.VMEM((OWNED * 4 * LOCAL_TERMS * B, 2 * B), BF16),
                pltpu.VMEM((OWNED, 2 * B, 2 * B), BF16),
                pltpu.VMEM((OWNED, B, B), F32),
                pltpu.VMEM((OWNED, B, B), F32),
            ],
        ),
        compiler_params=pltpu.CompilerParams(
            dimension_semantics=("arbitrary",), vmem_limit_bytes=40 << 20
        ),
        cost_estimate=pl.CostEstimate(
            flops=5 * 128 * 4 * 2 * B**3, bytes_accessed=6 << 20, transcendentals=0
        ),
        name="krylov",
    )(place, sizes, psi, *alphas, *betas)


def davidson_kernel(volume, place_ref, report_ref, basis_ref, out_ref, energy_ref):
    odd = lax.rem(place_ref[0], 2) == 1
    group = place_ref[1]
    report = report_ref[...]
    row_8, lane_8 = iotas(8)

    def column(slot):
        return jnp.sum(jnp.where(lane_8 == slot, report, 0.0), axis=1, keepdims=True)

    weight = column(0)
    alphas = [column(1 + i) for i in range(NVEC - 1)]
    betas = [column(NVEC + i) for i in range(NVEC - 1)]
    gram = {}
    slot = 1 + 2 * (NVEC - 1)
    for i in range(NVEC):
        for j in range(i, NVEC):
            gram[i, j] = gram[j, i] = column(slot)
            slot += 1

    def mean_dot(first, second):
        parts = None
        for i, a in enumerate(first):
            inner = None
            for j, b in enumerate(second):
                piece = gram[i, j] * b
                inner = piece if inner is None else inner + piece
            piece = a * inner
            parts = piece if parts is None else parts + piece
        return jnp.sum(parts, axis=0, keepdims=True) / volume

    def apply_ham(vector):
        size = len(vector)
        out = []
        for i in range(size + 1):
            value = jnp.zeros((8, 1), F32)
            if i < size:
                value = value + alphas[i] * vector[i]
            if i >= 1:
                value = value + betas[i - 1] * vector[i - 1]
            if i + 1 < size:
                value = value + betas[i] * vector[i + 1]
            out.append(value)
        return out

    def combine(a, first, b, second):
        out = []
        for i in range(max(len(first), len(second))):
            value = None
            if i < len(first):
                value = a * first[i]
            if i < len(second):
                piece = b * second[i]
                value = piece if value is None else value + piece
            out.append(value)
        return out

    started = [weight]
    norm = jnp.sqrt(mean_dot(started, started) + epsilon)
    vector = [weight / norm]
    image = apply_ham(vector)
    energy = mean_dot(vector, image)
    for _ in range(ITERS):
        residual = combine(1.0, image, -energy, vector)
        norm = jnp.sqrt(mean_dot(residual, residual) + epsilon)
        along = mean_dot(residual, image) / norm
        unit = [value / norm for value in residual]
        image_unit = apply_ham(unit)
        curve = mean_dot(unit, image_unit)
        gap_half = 0.5 * (curve - energy)
        lowest = 0.5 * (curve + energy) - jnp.sqrt(gap_half * gap_half + along * along)
        coef_b = lowest - energy
        combined = jnp.sqrt(along * along + coef_b * coef_b)
        vector = combine(along / combined, vector, coef_b / combined, unit)
        image = combine(along / combined, image, coef_b / combined, image_unit)
        energy = lowest

    mine = lax.broadcasted_iota(jnp.int32, (8, 1), 0) == group
    coefs = [jnp.sum(jnp.where(mine, value, 0.0), axis=0, keepdims=True) for value in vector]
    for owned in range(OWNED):
        value = None
        for i, coef in enumerate(coefs):
            piece = coef * basis_ref[i, owned]
            value = piece if value is None else value + piece
        out_ref[0, owned] = jnp.where(odd, value.T, value)
    energy_ref[...] = jnp.broadcast_to(energy, (8, B))


def davidson(place, report, basis, volume):
    return pl.pallas_call(
        functools.partial(davidson_kernel, volume),
        out_shape=(
            jax.ShapeDtypeStruct((1, OWNED, B, B), F32),
            jax.ShapeDtypeStruct((8, B), F32),
        ),
        grid_spec=pltpu.PrefetchScalarGridSpec(
            num_scalar_prefetch=1,
            grid=(1,),
            in_specs=[
                pl.BlockSpec((8, B), lambda i, place: (0, 0)),
                pl.BlockSpec((NVEC - 1, OWNED, B, B), lambda i, place: (0, 0, 0, 0)),
            ],
            out_specs=(
                pl.BlockSpec((1, OWNED, B, B), lambda i, place: (0, 0, 0, 0)),
                pl.BlockSpec((8, B), lambda i, place: (0, 0)),
            ),
        ),
        compiler_params=pltpu.CompilerParams(dimension_semantics=("arbitrary",), vmem_limit_bytes=16 << 20),
        name="davidson",
    )(place, report, basis)


def exchange_pairs(segments, groups, partner, offset):
    return [
        (seg * groups + term, partner(seg) * groups + (term + offset) % groups)
        for seg in range(segments)
        for term in range(groups)
    ]


def local(segments, groups, psi_guess, transfer_raw, left_env, right_env, block_sizes):
    place = jnp.stack([lax.axis_index("chain"), lax.axis_index("term")]).astype(jnp.int32)

    def alpha_partner(seg):
        if seg in (0, segments - 1):
            return seg
        return seg + 1 if seg % 2 else seg - 1

    def beta_partner(seg):
        return seg ^ 1

    alphas, betas = [None] * groups, [None] * groups
    for offset in (2, 1, 3, 0):
        alpha, beta = dress(place, left_env, right_env, transfer_raw, offset, segments, groups)
        for value, partner, store in ((alpha, alpha_partner, alphas), (beta, beta_partner, betas)):
            pairs = exchange_pairs(segments, groups, partner, offset)
            store[offset] = lax.ppermute(value, ("chain", "term"), pairs)
    volume = float(psi_guess.shape[1] * B * B)
    basis, report = krylov(place, block_sizes, psi_guess, alphas, betas)
    report = lax.psum(report, "term")
    vector, energy = davidson(place, report, basis, volume)
    return vector, energy[0, :1]


def solution(mesh):
    segments, groups = mesh.shape["chain"], mesh.shape["term"]
    placed = (
        P("chain", None, None, None),
        P("chain", None, None, None),
        P("chain", "term", None, None, None),
        P("chain", "term", None, None, None),
        P("chain", None, None),
    )
    return jax.shard_map(
        functools.partial(local, segments, groups),
        mesh=mesh,
        in_specs=placed,
        out_specs=(P("chain", "term", None, None), P("chain")),
        check_vma=False,
    )
```

```python
import functools
import math

import jax
import jax.numpy as jnp
from jax import lax
from jax.experimental import pallas as pl
from jax.experimental.pallas import tpu as pltpu
from jax.sharding import PartitionSpec as P

ITERS = 4
NVEC = ITERS + 2
twist_scale = 0.22
shrink = 1.047
epsilon = 1e-06

B = 128
HALF = 64
F32 = jnp.float32
BF16 = jnp.bfloat16

OWNED = 2
LOCAL_TERMS = 8
MATS = OWNED * LOCAL_TERMS
DIAG_ROW = MATS * HALF
MSG_ROWS = DIAG_ROW + MATS // 2


def split(value):
    high = value.astype(BF16)
    low = (value - high.astype(F32)).astype(BF16)
    return high, low


def dot(left, right):
    return jnp.dot(left, right, preferred_element_type=F32)


def iotas(rows):
    row = lax.broadcasted_iota(jnp.int32, (rows, B), 0)
    lane = lax.broadcasted_iota(jnp.int32, (rows, B), 1)
    return row, lane


def swap_halves(value):
    return pltpu.roll(value, HALF, 1)


def dress_kernel(segments, place_ref, left_ref, right_ref, raw_ref, alpha_ref, beta_ref):
    step = pl.program_id(0)
    seg = place_ref[0]
    odd = lax.rem(seg, 2) == 1
    edge = jnp.logical_or(seg == 0, seg == segments - 1)
    alpha_left = jnp.logical_xor(odd, edge)
    beta_left = jnp.logical_not(odd)

    raw = raw_ref[0, 0]
    skew = (raw - raw.T) * (twist_scale / math.sqrt(2.0 * B) / shrink)
    row, lane = iotas(B)
    eye = jnp.where(row == lane, 1.0, 0.0).astype(F32)
    sign = jnp.where(odd, 1.0, -1.0).astype(F32)
    diag_a = jnp.where(edge, 1.0, 1.0 / shrink).astype(F32)
    skew_a = jnp.where(edge, 0.0, sign).astype(F32)

    def factors(diag, coef):
        even, odd_part = eye * diag, skew * coef
        high, low = split((even + odd_part) * 0.5)
        right_op = jnp.concatenate([jnp.concatenate([high, low], 1)] * 2, 0)
        high, low = split(even - odd_part)
        left_op = jnp.concatenate([jnp.concatenate([high] * 2, 1), jnp.concatenate([low] * 2, 1)], 0)
        return left_op, right_op

    row_h, lane_h = iotas(HALF)
    keep_top = jnp.logical_or(lane_h >= HALF, lane_h >= row_h)
    on_diag_high = lane_h - HALF == row_h
    on_diag_low = lane_h == row_h

    sides = (
        (alpha_left, factors(diag_a, skew_a), alpha_ref),
        (beta_left, factors(F32(1.0 / shrink), -sign), beta_ref),
    )
    work = [(side, pair) for side in range(2) for pair in range(2)]
    parts = []
    for side, pair in work:
        take_left, (_, right_op), _ = sides[side]
        rows = []
        for term in (2 * pair, 2 * pair + 1):
            env = jnp.where(take_left, left_ref[0, term, 0], right_ref[0, term, 0])
            high, low = split(env + env.T)
            rows.append(jnp.concatenate([high, low], 1))
        parts.append(dot(jnp.concatenate(rows, 0), right_op))
    fulls = []
    for (side, pair), part in zip(work, parts):
        high, low = split(part[:, :B] + part[:, B:])
        right_side = jnp.concatenate(
            [jnp.concatenate([high[:B], high[B:]], 1), jnp.concatenate([low[:B], low[B:]], 1)], 0
        )
        full = dot(sides[side][1][0], right_side)
        fulls.append(full[:B] + full[B:])
    for (side, pair), full in zip(work, fulls):
        out_ref = sides[side][2]
        diag = jnp.zeros((HALF, B), F32)
        for j in range(2):
            mat = full[:, j * B : (j + 1) * B]
            top, bottom = mat[:HALF], mat[HALF:]
            turned = swap_halves(bottom)
            start = pl.multiple_of((step * 4 + 2 * pair + j) * HALF, HALF)
            out_ref[pl.ds(start, HALF), :] = jnp.where(keep_top, top, turned)
            if j == 0:
                diag = jnp.where(on_diag_high, bottom, diag)
            else:
                diag = jnp.where(on_diag_low, turned, diag)
        out_ref[pl.ds(DIAG_ROW + step * 2 + pair, 1), :] = jnp.sum(diag, axis=0, keepdims=True)


def dress(place, left_env, right_env, raw, offset, segments, groups):
    def env_map(step, place):
        sector = OWNED * lax.rem(place[1] + offset, groups) + step // 2
        return (0, lax.rem(step, 2), sector, 0, 0)

    def raw_map(step, place):
        return (0, OWNED * lax.rem(place[1] + offset, groups) + step // 2, 0, 0)

    out = jax.ShapeDtypeStruct((MSG_ROWS, B), F32)
    whole = pl.BlockSpec((MSG_ROWS, B), lambda step, place: (0, 0))
    return pl.pallas_call(
        functools.partial(dress_kernel, segments),
        out_shape=(out, out),
        grid_spec=pltpu.PrefetchScalarGridSpec(
            num_scalar_prefetch=1,
            grid=(4,),
            in_specs=[
                pl.BlockSpec((1, 4, 1, B, B), env_map),
                pl.BlockSpec((1, 4, 1, B, B), env_map),
                pl.BlockSpec((1, 1, B, B), raw_map),
            ],
            out_specs=(whole, whole),
        ),
        compiler_params=pltpu.CompilerParams(
            dimension_semantics=("arbitrary",), vmem_limit_bytes=58 << 20
        ),
        cost_estimate=pl.CostEstimate(flops=1000, bytes_accessed=1000, transcendentals=0),
        name="dress",
    )(place, left_env, right_env, raw)


def total(value):
    tiles = jnp.sum(value.reshape(OWNED * B // 8, 8, B), axis=0)
    return jnp.sum(jnp.sum(tiles, axis=0, keepdims=True), axis=1, keepdims=True)


def unpack(msg_ref, pairs):
    row_h, lane_h = iotas(HALF)
    keep_top = jnp.logical_or(lane_h >= HALF, lane_h >= row_h)
    keep_bottom = jnp.logical_and(lane_h >= HALF, lane_h - HALF < row_h)
    on_diag = lane_h - HALF == row_h
    packed = [msg_ref[2 * pair * HALF : (2 * pair + 2) * HALF, :] for pair in pairs]
    diags = [msg_ref[DIAG_ROW + pair : DIAG_ROW + pair + 1, :] for pair in pairs]
    out = []
    for pair_value, diag_row in zip(packed, diags):
        for j in range(2):
            value = pair_value[j * HALF : (j + 1) * HALF]
            turned = swap_halves(value)
            flipped = jnp.concatenate([value, turned], 0).T
            diag = diag_row if j == 0 else swap_halves(diag_row)
            top = jnp.where(keep_top, value, flipped[:HALF])
            bottom = jnp.where(keep_bottom, turned, flipped[HALF:])
            bottom = jnp.where(on_diag, jnp.broadcast_to(diag, (HALF, B)), bottom)
            high, low = split(jnp.concatenate([top, bottom], 0))
            out.append(jnp.concatenate([high, low], 1))
    return out


def doubled(vector):
    high, low = split(vector)
    return jnp.concatenate([jnp.concatenate([high, low], 1)] * 2, 0)


def between(half):
    high, low = split(half[:, :B] + half[:, B:])
    return jnp.concatenate(
        [jnp.concatenate([high[:B], high[B:]], 1), jnp.concatenate([low[:B], low[B:]], 1)], 0
    )


def quarters(out):
    return (out[:B, :B] + out[:B, B:]) + (out[B:, :B] + out[B:, B:])


def live_mask(place_ref, sizes_ref, owned):
    odd = lax.rem(place_ref[0], 2) == 1
    row, lane = iotas(B)
    rows_live = sizes_ref[0, 0, OWNED * place_ref[1] + owned]
    cols_live = sizes_ref[0, 1, OWNED * place_ref[1] + owned]
    first = jnp.where(odd, cols_live, rows_live)
    second = jnp.where(odd, rows_live, cols_live)
    return jnp.where(jnp.logical_and(row < first, lane < second), 1.0, 0.0).astype(F32)


def start_vector(place_ref, sizes_ref, psi_ref, owned):
    odd = lax.rem(place_ref[0], 2) == 1
    guess = psi_ref[0, owned]
    return jnp.where(odd, guess.T, guess) * live_mask(place_ref, sizes_ref, owned)


def arrive_kernel(place_ref, sizes_ref, psi_ref, before_ref, alpha_ref, beta_ref, left_ref, right_ref, image_ref):
    per_sector = LOCAL_TERMS // 2
    for owned in range(OWNED):
        vector = doubled(start_vector(place_ref, sizes_ref, psi_ref, owned))
        pairs = [owned * per_sector + i for i in range(per_sector)]
        lefts = unpack(alpha_ref, pairs)
        rights = unpack(beta_ref, pairs)
        for i in range(LOCAL_TERMS):
            start = (owned * LOCAL_TERMS + i) * B
            left_ref[start : start + B, :] = lefts[i]
            right_ref[start : start + B, :] = rights[i]
        mids = [between(dot(jnp.concatenate(lefts[2 * i : 2 * i + 2], 0), vector)) for i in range(per_sector)]
        image = quarters(dot(jnp.concatenate(mids, 1), jnp.concatenate(rights, 0)))
        image_ref[owned] = before_ref[owned] + image


def arrive(place, sizes, psi, before, alpha, beta):
    rows = MATS * B
    message = pl.BlockSpec((MSG_ROWS, B), lambda i, place: (0, 0))
    block = pl.BlockSpec((rows, 2 * B), lambda i, place: (0, 0))
    return pl.pallas_call(
        arrive_kernel,
        out_shape=(
            jax.ShapeDtypeStruct((rows, 2 * B), BF16),
            jax.ShapeDtypeStruct((rows, 2 * B), BF16),
            jax.ShapeDtypeStruct((OWNED, B, B), F32),
        ),
        grid_spec=pltpu.PrefetchScalarGridSpec(
            num_scalar_prefetch=1,
            grid=(1,),
            in_specs=[
                pl.BlockSpec(memory_space=pltpu.SMEM),
                pl.BlockSpec((1, OWNED, B, B), lambda i, place: (0, place[1], 0, 0)),
                pl.BlockSpec((OWNED, B, B), lambda i, place: (0, 0, 0)),
                message,
                message,
            ],
            out_specs=(block, block, pl.BlockSpec((OWNED, B, B), lambda i, place: (0, 0, 0))),
        ),
        compiler_params=pltpu.CompilerParams(
            dimension_semantics=("arbitrary",), vmem_limit_bytes=20 << 20
        ),
        cost_estimate=pl.CostEstimate(flops=1000, bytes_accessed=1000, transcendentals=0),
        name="arrive",
    )(place, sizes, psi, before, alpha, beta)


def krylov_kernel(place_ref, sizes_ref, psi_ref, *refs):
    lefts, rights, image_ref = refs[0:4], refs[4:8], refs[8]
    basis_ref, report_ref = refs[9:11]
    vec_ref, acc_ref, mask_ref = refs[11:]
    group = place_ref[1]
    starts = []
    for owned in range(OWNED):
        mask_ref[owned] = live_mask(place_ref, sizes_ref, owned)
        starts.append(start_vector(place_ref, sizes_ref, psi_ref, owned))
    vector = jnp.stack(starts, 0)

    def apply_ham():
        acc_ref[...] = jnp.zeros_like(acc_ref)

        def body(index, carry):
            units = []
            for owned in range(OWNED):
                start = pl.multiple_of((owned * (LOCAL_TERMS // 2) + index) * 2 * B, 2 * B)
                units.append([between(dot(left[pl.ds(start, 2 * B), :], vec_ref[owned])) for left in lefts])
            for owned in range(OWNED):
                start = pl.multiple_of((owned * (LOCAL_TERMS // 2) + index) * 2 * B, 2 * B)
                right = jnp.concatenate([ref[pl.ds(start, 2 * B), :] for ref in rights], 0)
                acc_ref[owned] += quarters(dot(jnp.concatenate(units[owned], 1), right))
            return carry

        lax.fori_loop(0, LOCAL_TERMS // 2, body, 0)
        return acc_ref[...] * mask_ref[...]

    def inverse_norm(square):
        return jnp.where(square > 0.0, lax.rsqrt(jnp.where(square > 0.0, square, 1.0)), 0.0)

    lane_1 = lax.broadcasted_iota(jnp.int32, (1, B), 1)
    report = jnp.zeros((1, B), F32)

    def put(report, slot, value):
        return jnp.where(lane_1 == slot, value, report)

    square = total(vector * vector)
    scale = inverse_norm(square)
    report = put(report, 0, square * scale)
    basis_ref[0] = vector * scale
    previous_beta = None
    for step in range(NVEC - 1):
        current = basis_ref[step]
        if step:
            for owned in range(OWNED):
                vec_ref[owned] = doubled(current[owned])
            image = apply_ham()
        else:
            image = image_ref[...] * mask_ref[...] * scale
        alpha = total(current * image)
        rest = image - alpha * current
        if step:
            rest = rest - previous_beta * basis_ref[step - 1]
        square = total(rest * rest)
        scale = inverse_norm(square)
        beta = square * scale
        basis_ref[step + 1] = rest * scale
        report = put(report, 1 + step, alpha)
        report = put(report, 1 + (NVEC - 1) + step, beta)
        previous_beta = beta
    slot = 1 + 2 * (NVEC - 1)
    for i in range(NVEC):
        for j in range(i, NVEC):
            report = put(report, slot, total(basis_ref[i] * basis_ref[j]))
            slot += 1
    row_8, _ = iotas(8)
    report_ref[...] = jnp.where(row_8 == group, jnp.broadcast_to(report, (8, B)), 0.0)


def krylov(place, sizes, psi, lefts, rights, image):
    block = pl.BlockSpec((MATS * B, 2 * B), lambda i, place: (0, 0))
    return pl.pallas_call(
        krylov_kernel,
        out_shape=(
            jax.ShapeDtypeStruct((NVEC, OWNED, B, B), F32),
            jax.ShapeDtypeStruct((8, B), F32),
        ),
        grid_spec=pltpu.PrefetchScalarGridSpec(
            num_scalar_prefetch=1,
            grid=(1,),
            in_specs=[
                pl.BlockSpec(memory_space=pltpu.SMEM),
                pl.BlockSpec((1, OWNED, B, B), lambda i, place: (0, place[1], 0, 0)),
            ]
            + [block] * 8
            + [pl.BlockSpec((OWNED, B, B), lambda i, place: (0, 0, 0))],
            out_specs=(
                pl.BlockSpec((NVEC, OWNED, B, B), lambda i, place: (0, 0, 0, 0)),
                pl.BlockSpec((8, B), lambda i, place: (0, 0)),
            ),
            scratch_shapes=[
                pltpu.VMEM((OWNED, 2 * B, 2 * B), BF16),
                pltpu.VMEM((OWNED, B, B), F32),
                pltpu.VMEM((OWNED, B, B), F32),
            ],
        ),
        compiler_params=pltpu.CompilerParams(
            dimension_semantics=("arbitrary",), vmem_limit_bytes=28 << 20
        ),
        cost_estimate=pl.CostEstimate(
            flops=4 * 128 * 4 * 2 * B**3, bytes_accessed=9 << 20, transcendentals=0
        ),
        name="krylov",
    )(place, sizes, psi, *lefts, *rights, image)


def davidson_kernel(volume, place_ref, report_ref, basis_ref, out_ref, energy_ref):
    odd = lax.rem(place_ref[0], 2) == 1
    group = place_ref[1]
    report = report_ref[...]
    row_8, lane_8 = iotas(8)

    def column(slot):
        return jnp.sum(jnp.where(lane_8 == slot, report, 0.0), axis=1, keepdims=True)

    weight = column(0)
    alphas = [column(1 + i) for i in range(NVEC - 1)]
    betas = [column(NVEC + i) for i in range(NVEC - 1)]
    gram = {}
    slot = 1 + 2 * (NVEC - 1)
    for i in range(NVEC):
        for j in range(i, NVEC):
            gram[i, j] = gram[j, i] = column(slot)
            slot += 1

    def mean_dot(first, second):
        parts = None
        for i, a in enumerate(first):
            inner = None
            for j, b in enumerate(second):
                piece = gram[i, j] * b
                inner = piece if inner is None else inner + piece
            piece = a * inner
            parts = piece if parts is None else parts + piece
        return jnp.sum(parts, axis=0, keepdims=True) / volume

    def apply_ham(vector):
        size = len(vector)
        out = []
        for i in range(size + 1):
            value = jnp.zeros((8, 1), F32)
            if i < size:
                value = value + alphas[i] * vector[i]
            if i >= 1:
                value = value + betas[i - 1] * vector[i - 1]
            if i + 1 < size:
                value = value + betas[i] * vector[i + 1]
            out.append(value)
        return out

    def combine(a, first, b, second):
        out = []
        for i in range(max(len(first), len(second))):
            value = None
            if i < len(first):
                value = a * first[i]
            if i < len(second):
                piece = b * second[i]
                value = piece if value is None else value + piece
            out.append(value)
        return out

    started = [weight]
    norm = jnp.sqrt(mean_dot(started, started) + epsilon)
    vector = [weight / norm]
    image = apply_ham(vector)
    energy = mean_dot(vector, image)
    for _ in range(ITERS):
        residual = combine(1.0, image, -energy, vector)
        norm = jnp.sqrt(mean_dot(residual, residual) + epsilon)
        along = mean_dot(residual, image) / norm
        unit = [value / norm for value in residual]
        image_unit = apply_ham(unit)
        curve = mean_dot(unit, image_unit)
        gap_half = 0.5 * (curve - energy)
        lowest = 0.5 * (curve + energy) - jnp.sqrt(gap_half * gap_half + along * along)
        coef_b = lowest - energy
        combined = jnp.sqrt(along * along + coef_b * coef_b)
        vector = combine(along / combined, vector, coef_b / combined, unit)
        image = combine(along / combined, image, coef_b / combined, image_unit)
        energy = lowest

    mine = lax.broadcasted_iota(jnp.int32, (8, 1), 0) == group
    coefs = [jnp.sum(jnp.where(mine, value, 0.0), axis=0, keepdims=True) for value in vector]
    for owned in range(OWNED):
        value = None
        for i, coef in enumerate(coefs):
            piece = coef * basis_ref[i, owned]
            value = piece if value is None else value + piece
        out_ref[0, owned] = jnp.where(odd, value.T, value)
    energy_ref[...] = jnp.broadcast_to(energy, (8, B))


def davidson(place, report, basis, volume):
    return pl.pallas_call(
        functools.partial(davidson_kernel, volume),
        out_shape=(
            jax.ShapeDtypeStruct((1, OWNED, B, B), F32),
            jax.ShapeDtypeStruct((8, B), F32),
        ),
        grid_spec=pltpu.PrefetchScalarGridSpec(
            num_scalar_prefetch=1,
            grid=(1,),
            in_specs=[
                pl.BlockSpec((8, B), lambda i, place: (0, 0)),
                pl.BlockSpec((NVEC - 1, OWNED, B, B), lambda i, place: (0, 0, 0, 0)),
            ],
            out_specs=(
                pl.BlockSpec((1, OWNED, B, B), lambda i, place: (0, 0, 0, 0)),
                pl.BlockSpec((8, B), lambda i, place: (0, 0)),
            ),
        ),
        compiler_params=pltpu.CompilerParams(dimension_semantics=("arbitrary",), vmem_limit_bytes=16 << 20),
        name="davidson",
    )(place, report, basis)


def exchange_pairs(segments, groups, partner, offset):
    return [
        (seg * groups + term, partner(seg) * groups + (term + offset) % groups)
        for seg in range(segments)
        for term in range(groups)
    ]


def local(segments, groups, psi_guess, transfer_raw, left_env, right_env, block_sizes):
    place = jnp.stack([lax.axis_index("chain"), lax.axis_index("term")]).astype(jnp.int32)

    def alpha_partner(seg):
        if seg in (0, segments - 1):
            return seg
        return seg + 1 if seg % 2 else seg - 1

    def beta_partner(seg):
        return seg ^ 1

    messages = []
    for offset in (2, 1, 3, 0):
        alpha, beta = dress(place, left_env, right_env, transfer_raw, offset, segments, groups)
        alpha, beta, place = lax.optimization_barrier((alpha, beta, place))
        messages.append((offset, alpha, beta))
    lefts, rights = [], []
    image = jnp.zeros((OWNED, B, B), F32)
    for offset, alpha, beta in messages:
        alpha = lax.ppermute(alpha, ("chain", "term"), exchange_pairs(segments, groups, alpha_partner, offset))
        beta = lax.ppermute(beta, ("chain", "term"), exchange_pairs(segments, groups, beta_partner, offset))
        left, right, image = arrive(place, block_sizes, psi_guess, image, alpha, beta)
        lefts.append(left)
        rights.append(right)
    volume = float(psi_guess.shape[1] * B * B)
    basis, report = krylov(place, block_sizes, psi_guess, lefts, rights, image)
    report = lax.psum(report, "term")
    vector, energy = davidson(place, report, basis, volume)
    return vector, energy[0, :1]


def solution(mesh):
    segments, groups = mesh.shape["chain"], mesh.shape["term"]
    placed = (
        P("chain", None, None, None),
        P("chain", None, None, None),
        P("chain", "term", None, None, None),
        P("chain", "term", None, None, None),
        P("chain", None, None),
    )
    return jax.shard_map(
        functools.partial(local, segments, groups),
        mesh=mesh,
        in_specs=placed,
        out_specs=(P("chain", "term", None, None), P("chain")),
        check_vma=False,
    )
```

```python
import functools
import math

import jax
import jax.numpy as jnp
from jax import lax
from jax.experimental import pallas as pl
from jax.experimental.pallas import tpu as pltpu
from jax.sharding import PartitionSpec as P

ITERS = 4
NVEC = ITERS + 2
twist_scale = 0.22
shrink = 1.047
epsilon = 1e-06

B = 128
HALF = 64
F32 = jnp.float32
BF16 = jnp.bfloat16

OWNED = 2
LOCAL_TERMS = 8
MATS = OWNED * LOCAL_TERMS
DIAG_ROW = MATS * HALF
MSG_ROWS = DIAG_ROW + MATS // 2


def split(value):
    high = value.astype(BF16)
    low = (value - high.astype(F32)).astype(BF16)
    return high, low


def dot(left, right):
    return jnp.dot(left, right, preferred_element_type=F32)


def iotas(rows):
    row = lax.broadcasted_iota(jnp.int32, (rows, B), 0)
    lane = lax.broadcasted_iota(jnp.int32, (rows, B), 1)
    return row, lane


def swap_halves(value):
    return pltpu.roll(value, HALF, 1)


def dress_kernel(segments, groups, jobs, left_hbm, right_hbm, raw_hbm, *refs):
    outs, (env_ref, raw_ref, env_sem, raw_sem) = refs[: len(jobs)], refs[len(jobs) :]
    seg = lax.axis_index("chain")
    odd = lax.rem(seg, 2) == 1
    edge = jnp.logical_or(seg == 0, seg == segments - 1)

    def first_sector(slot):
        return OWNED * lax.rem(lax.axis_index("term") + jobs[slot][1], groups)

    def env_copy(source, slot, owned):
        part = source.at[0, :, first_sector(slot) + owned]
        return pltpu.make_async_copy(part, env_ref.at[slot, owned], env_sem.at[slot, owned])

    def raw_copy(slot):
        part = raw_hbm.at[0, pl.ds(first_sector(slot), OWNED)]
        return pltpu.make_async_copy(part, raw_ref.at[slot], raw_sem.at[slot])

    for slot, (side, _) in enumerate(jobs):
        raw_copy(slot).start()
        take_left = jnp.logical_not(odd) if side else jnp.logical_xor(odd, edge)

        @pl.when(take_left)
        def _():
            for owned in range(OWNED):
                env_copy(left_hbm, slot, owned).start()

        @pl.when(jnp.logical_not(take_left))
        def _():
            for owned in range(OWNED):
                env_copy(right_hbm, slot, owned).start()

    row, lane = iotas(B)
    eye = jnp.where(row == lane, 1.0, 0.0).astype(F32)
    sign = jnp.where(odd, 1.0, -1.0).astype(F32)
    row_h, lane_h = iotas(HALF)
    keep_top = jnp.logical_or(lane_h >= HALF, lane_h >= row_h)
    on_diag_high = lane_h - HALF == row_h
    on_diag_low = lane_h == row_h
    pairs = LOCAL_TERMS // 2
    for slot, (side, _) in enumerate(jobs):
        raw_copy(slot).wait()
        out_ref = outs[slot]
        if side:
            even, coef = eye * (1.0 / shrink), -sign
        else:
            even = eye * jnp.where(edge, 1.0, 1.0 / shrink).astype(F32)
            coef = jnp.where(edge, 0.0, sign).astype(F32)
        coef = coef * (twist_scale / math.sqrt(2.0 * B) / shrink)
        factors = []
        for owned in range(OWNED):
            raw = raw_ref[slot, owned]
            odd_part = (raw - raw.T) * coef
            high, low = split((even + odd_part) * 0.5)
            right_op = jnp.concatenate([jnp.concatenate([high, low], 1)] * 2, 0)
            high, low = split(even - odd_part)
            left_op = jnp.concatenate([jnp.concatenate([high] * 2, 1), jnp.concatenate([low] * 2, 1)], 0)
            factors.append((left_op, right_op))
        for owned in range(OWNED):
            env_copy(left_hbm, slot, owned).wait()
        work = [(owned, pair) for owned in range(OWNED) for pair in range(pairs)]
        parts = []
        for owned, pair in work:
            sums = []
            for term in (2 * pair, 2 * pair + 1):
                env = env_ref[slot, owned, term]
                high, low = split(env + env.T)
                sums.append(jnp.concatenate([high, low], 1))
            parts.append(dot(jnp.concatenate(sums, 0), factors[owned][1]))
        fulls = []
        for (owned, pair), part in zip(work, parts):
            high, low = split(part[:, :B] + part[:, B:])
            right_side = jnp.concatenate(
                [jnp.concatenate([high[:B], high[B:]], 1), jnp.concatenate([low[:B], low[B:]], 1)], 0
            )
            full = dot(factors[owned][0], right_side)
            fulls.append(full[:B] + full[B:])
        for index, full in enumerate(fulls):
            diag = jnp.zeros((HALF, B), F32)
            for j in range(2):
                mat = full[:, j * B : (j + 1) * B]
                top, bottom = mat[:HALF], mat[HALF:]
                turned = swap_halves(bottom)
                start = (2 * index + j) * HALF
                out_ref[start : start + HALF, :] = jnp.where(keep_top, top, turned)
                if j == 0:
                    diag = jnp.where(on_diag_high, bottom, diag)
                else:
                    diag = jnp.where(on_diag_low, turned, diag)
            start = DIAG_ROW + index
            out_ref[start : start + 1, :] = jnp.sum(diag, axis=0, keepdims=True)


TINY = pl.CostEstimate(flops=1000, bytes_accessed=1000, transcendentals=0)
VMEM = pl.BlockSpec(memory_space=pltpu.VMEM)
SMEM = pl.BlockSpec(memory_space=pltpu.SMEM)
BLOCK_ROWS = MATS * B


def dress(left_env, right_env, raw, jobs, segments, groups, limit):
    count = len(jobs)
    return pl.pallas_call(
        functools.partial(dress_kernel, segments, groups, jobs),
        out_shape=(jax.ShapeDtypeStruct((MSG_ROWS, B), F32),) * count,
        in_specs=[pl.BlockSpec(memory_space=pltpu.HBM)] * 3,
        out_specs=(VMEM,) * count,
        scratch_shapes=[
            pltpu.VMEM((count, OWNED, LOCAL_TERMS, B, B), F32),
            pltpu.VMEM((count, OWNED, B, B), F32),
            pltpu.SemaphoreType.DMA((count, OWNED)),
            pltpu.SemaphoreType.DMA((count,)),
        ],
        compiler_params=pltpu.CompilerParams(vmem_limit_bytes=limit << 20),
        cost_estimate=TINY,
        name="dress",
    )(left_env, right_env, raw)


def total(value):
    tiles = jnp.sum(value.reshape(OWNED * B // 8, 8, B), axis=0)
    return jnp.sum(jnp.sum(tiles, axis=0, keepdims=True), axis=1, keepdims=True)


def unpack(msg_ref, pairs):
    row_h, lane_h = iotas(HALF)
    keep_top = jnp.logical_or(lane_h >= HALF, lane_h >= row_h)
    keep_bottom = jnp.logical_and(lane_h >= HALF, lane_h - HALF < row_h)
    on_diag = lane_h - HALF == row_h
    packed = [msg_ref[2 * pair * HALF : (2 * pair + 2) * HALF, :] for pair in pairs]
    diags = [msg_ref[DIAG_ROW + pair : DIAG_ROW + pair + 1, :] for pair in pairs]
    out = []
    for pair_value, diag_row in zip(packed, diags):
        for j in range(2):
            value = pair_value[j * HALF : (j + 1) * HALF]
            turned = swap_halves(value)
            flipped = jnp.concatenate([value, turned], 0).T
            diag = diag_row if j == 0 else swap_halves(diag_row)
            top = jnp.where(keep_top, value, flipped[:HALF])
            bottom = jnp.where(keep_bottom, turned, flipped[HALF:])
            bottom = jnp.where(on_diag, jnp.broadcast_to(diag, (HALF, B)), bottom)
            high, low = split(jnp.concatenate([top, bottom], 0))
            out.append(jnp.concatenate([high, low], 1))
    return out


def doubled(vector):
    high, low = split(vector)
    return jnp.concatenate([jnp.concatenate([high, low], 1)] * 2, 0)


def between(half):
    high, low = split(half[:, :B] + half[:, B:])
    return jnp.concatenate(
        [jnp.concatenate([high[:B], high[B:]], 1), jnp.concatenate([low[:B], low[B:]], 1)], 0
    )


def quarters(out):
    return (out[:B, :B] + out[:B, B:]) + (out[B:, :B] + out[B:, B:])


def live_mask(sizes_ref, owned):
    odd = lax.rem(lax.axis_index("chain"), 2) == 1
    sector = OWNED * lax.axis_index("term") + owned
    row, lane = iotas(B)
    rows_live = sizes_ref[0, 0, sector]
    cols_live = sizes_ref[0, 1, sector]
    first = jnp.where(odd, cols_live, rows_live)
    second = jnp.where(odd, rows_live, cols_live)
    return jnp.where(jnp.logical_and(row < first, lane < second), 1.0, 0.0).astype(F32)


def start_vector(sizes_ref, psi_ref, owned):
    odd = lax.rem(lax.axis_index("chain"), 2) == 1
    guess = psi_ref[0, OWNED * lax.axis_index("term") + owned]
    return jnp.where(odd, guess.T, guess) * live_mask(sizes_ref, owned)


def arrive_kernel(sizes_ref, psi_ref, before_ref, alpha_ref, beta_ref, left_ref, right_ref, image_ref):
    pairs = LOCAL_TERMS // 2
    for owned in range(OWNED):
        vector = doubled(start_vector(sizes_ref, psi_ref, owned))
        which = [owned * pairs + i for i in range(pairs)]
        rows = slice(owned * LOCAL_TERMS * B, (owned + 1) * LOCAL_TERMS * B)
        lefts = unpack(alpha_ref, which)
        left_ref[rows, :] = jnp.concatenate(lefts, 0)
        mids = [between(dot(jnp.concatenate(lefts[2 * i : 2 * i + 2], 0), vector)) for i in range(pairs)]
        rights = jnp.concatenate(unpack(beta_ref, which), 0)
        right_ref[rows, :] = rights
        image_ref[owned] = before_ref[owned] + quarters(dot(jnp.concatenate(mids, 1), rights))


def arrive(sizes, psi, before, alpha, beta):
    block = jax.ShapeDtypeStruct((BLOCK_ROWS, 2 * B), BF16)
    return pl.pallas_call(
        arrive_kernel,
        out_shape=(block, block, jax.ShapeDtypeStruct((OWNED, B, B), F32)),
        in_specs=[SMEM] + [VMEM] * 4,
        out_specs=(VMEM,) * 3,
        compiler_params=pltpu.CompilerParams(vmem_limit_bytes=16 << 20),
        cost_estimate=TINY,
        name="arrive",
    )(sizes, psi, before, alpha, beta)


def krylov_kernel(sizes_ref, psi_ref, *refs):
    lefts, rights, image_ref = refs[0:4], refs[4:8], refs[8]
    basis_ref, report_ref = refs[9:11]
    vec_ref, acc_ref, mask_ref = refs[11:]
    group = lax.axis_index("term")
    starts = []
    for owned in range(OWNED):
        mask_ref[owned] = live_mask(sizes_ref, owned)
        starts.append(start_vector(sizes_ref, psi_ref, owned))
    vector = jnp.stack(starts, 0)

    def apply_ham():
        acc_ref[...] = jnp.zeros_like(acc_ref)

        def body(index, carry):
            units = []
            for owned in range(OWNED):
                start = pl.multiple_of((owned * (LOCAL_TERMS // 2) + index) * 2 * B, 2 * B)
                units.append([between(dot(left[pl.ds(start, 2 * B), :], vec_ref[owned])) for left in lefts])
            for owned in range(OWNED):
                start = pl.multiple_of((owned * (LOCAL_TERMS // 2) + index) * 2 * B, 2 * B)
                right = jnp.concatenate([ref[pl.ds(start, 2 * B), :] for ref in rights], 0)
                acc_ref[owned] += quarters(dot(jnp.concatenate(units[owned], 1), right))
            return carry

        lax.fori_loop(0, LOCAL_TERMS // 2, body, 0, unroll=True)
        return acc_ref[...] * mask_ref[...]

    def inverse_norm(square):
        return jnp.where(square > 0.0, lax.rsqrt(jnp.where(square > 0.0, square, 1.0)), 0.0)

    lane_1 = lax.broadcasted_iota(jnp.int32, (1, B), 1)
    report = jnp.zeros((1, B), F32)

    def put(report, slot, value):
        return jnp.where(lane_1 == slot, value, report)

    grams = []

    def partial_dot(first, second):
        return jnp.sum((first * second).reshape(OWNED * B, B), axis=0, keepdims=True)

    square = total(vector * vector)
    scale = inverse_norm(square)
    report = put(report, 0, square * scale)
    basis_ref[0] = vector * scale
    previous_beta = None
    for step in range(NVEC - 1):
        current = basis_ref[step]
        if step:
            for owned in range(OWNED):
                vec_ref[owned] = doubled(current[owned])
            image = apply_ham()
        else:
            image = image_ref[...] * mask_ref[...] * scale
        alpha = total(current * image)
        rest = image - alpha * current
        if step:
            rest = rest - previous_beta * basis_ref[step - 1]
        square = total(rest * rest)
        scale = inverse_norm(square)
        beta = square * scale
        basis_ref[step + 1] = rest * scale
        grams += [partial_dot(basis_ref[step], basis_ref[i]) for i in range(step + 1)]
        report = put(report, 1 + step, alpha)
        report = put(report, 1 + (NVEC - 1) + step, beta)
        previous_beta = beta
    grams += [partial_dot(basis_ref[NVEC - 1], basis_ref[i]) for i in range(NVEC)]
    first = 1 + 2 * (NVEC - 1)
    rows = [jnp.zeros((1, B), F32)] * first + grams
    rows += [jnp.zeros((1, B), F32)] * (B - len(rows))
    summed = jnp.sum(jnp.concatenate(rows, 0).T, axis=0, keepdims=True)
    report = report + summed
    row_8, _ = iotas(8)
    report_ref[...] = jnp.where(row_8 == group, jnp.broadcast_to(report, (8, B)), 0.0)


def krylov(sizes, psi, lefts, rights, image):
    return pl.pallas_call(
        krylov_kernel,
        out_shape=(
            jax.ShapeDtypeStruct((NVEC, OWNED, B, B), F32),
            jax.ShapeDtypeStruct((8, B), F32),
        ),
        in_specs=[SMEM] + [VMEM] * 10,
        out_specs=(VMEM, VMEM),
        scratch_shapes=[
            pltpu.VMEM((OWNED, 2 * B, 2 * B), BF16),
            pltpu.VMEM((OWNED, B, B), F32),
            pltpu.VMEM((OWNED, B, B), F32),
        ],
        compiler_params=pltpu.CompilerParams(vmem_limit_bytes=24 << 20),
        cost_estimate=TINY,
        name="krylov",
    )(sizes, psi, *lefts, *rights, image)


def davidson_kernel(volume, report_ref, basis_ref, out_ref, energy_ref):
    odd = lax.rem(lax.axis_index("chain"), 2) == 1
    group = lax.axis_index("term")
    report = report_ref[...]
    row_8, lane_8 = iotas(8)

    def column(slot):
        return jnp.sum(jnp.where(lane_8 == slot, report, 0.0), axis=1, keepdims=True)

    weight = column(0)
    alphas = [column(1 + i) for i in range(NVEC - 1)]
    betas = [column(NVEC + i) for i in range(NVEC - 1)]
    gram = {}
    slot = 1 + 2 * (NVEC - 1)
    for j in range(NVEC):
        for i in range(j + 1):
            gram[i, j] = gram[j, i] = column(slot)
            slot += 1

    def mean_dot(first, second):
        parts = None
        for i, a in enumerate(first):
            inner = None
            for j, b in enumerate(second):
                piece = gram[i, j] * b
                inner = piece if inner is None else inner + piece
            piece = a * inner
            parts = piece if parts is None else parts + piece
        return jnp.sum(parts, axis=0, keepdims=True) / volume

    def apply_ham(vector):
        size = len(vector)
        out = []
        for i in range(size + 1):
            value = jnp.zeros((8, 1), F32)
            if i < size:
                value = value + alphas[i] * vector[i]
            if i >= 1:
                value = value + betas[i - 1] * vector[i - 1]
            if i + 1 < size:
                value = value + betas[i] * vector[i + 1]
            out.append(value)
        return out

    def combine(a, first, b, second):
        out = []
        for i in range(max(len(first), len(second))):
            value = None
            if i < len(first):
                value = a * first[i]
            if i < len(second):
                piece = b * second[i]
                value = piece if value is None else value + piece
            out.append(value)
        return out

    started = [weight]
    norm = jnp.sqrt(mean_dot(started, started) + epsilon)
    vector = [weight / norm]
    image = apply_ham(vector)
    energy = mean_dot(vector, image)
    for _ in range(ITERS):
        residual = combine(1.0, image, -energy, vector)
        norm = jnp.sqrt(mean_dot(residual, residual) + epsilon)
        along = mean_dot(residual, image) / norm
        unit = [value / norm for value in residual]
        image_unit = apply_ham(unit)
        curve = mean_dot(unit, image_unit)
        gap_half = 0.5 * (curve - energy)
        lowest = 0.5 * (curve + energy) - jnp.sqrt(gap_half * gap_half + along * along)
        coef_b = lowest - energy
        combined = jnp.sqrt(along * along + coef_b * coef_b)
        vector = combine(along / combined, vector, coef_b / combined, unit)
        image = combine(along / combined, image, coef_b / combined, image_unit)
        energy = lowest

    mine = lax.broadcasted_iota(jnp.int32, (8, 1), 0) == group
    coefs = [jnp.sum(jnp.where(mine, value, 0.0), axis=0, keepdims=True) for value in vector]
    for owned in range(OWNED):
        value = None
        for i, coef in enumerate(coefs):
            piece = coef * basis_ref[i, owned]
            value = piece if value is None else value + piece
        out_ref[0, owned] = jnp.where(odd, value.T, value)
    energy_ref[0] = energy[0, 0]


def davidson(report, basis, volume):
    return pl.pallas_call(
        functools.partial(davidson_kernel, volume),
        out_shape=(
            jax.ShapeDtypeStruct((1, OWNED, B, B), F32),
            jax.ShapeDtypeStruct((1,), F32),
        ),
        in_specs=[VMEM, VMEM],
        out_specs=(VMEM, SMEM),
        compiler_params=pltpu.CompilerParams(vmem_limit_bytes=16 << 20),
        cost_estimate=TINY,
        name="davidson",
    )(report, basis)


ORDER = (
    (((0, 2), (1, 2)), 20),
    (((0, 1), (1, 1)), 20),
    (((0, 3), (1, 3)), 20),
    (((0, 0), (1, 0)), 20),
)


def exchange_pairs(segments, groups, partner, offset):
    return [
        (seg * groups + term, partner(seg) * groups + (term + offset) % groups)
        for seg in range(segments)
        for term in range(groups)
    ]


def local(segments, groups, psi_guess, transfer_raw, left_env, right_env, block_sizes):
    def alpha_partner(seg):
        if seg in (0, segments - 1):
            return seg
        return seg + 1 if seg % 2 else seg - 1

    def beta_partner(seg):
        return seg ^ 1

    partners = (alpha_partner, beta_partner)
    left_env, right_env, raw = [
        pltpu.with_memory_space_constraint(value, pltpu.HBM) for value in (left_env, right_env, transfer_raw)
    ]
    messages = {}
    for jobs, limit in ORDER:
        made = dress(left_env, right_env, raw, jobs, segments, groups, limit)
        made, raw = lax.optimization_barrier((made, raw))
        for job, message in zip(jobs, made):
            messages[job] = message

    def send(side, offset, after=None):
        message = messages[side, offset]
        if after is not None:
            message, _ = lax.optimization_barrier((message, after))
        return lax.ppermute(message, ("chain", "term"), exchange_pairs(segments, groups, partners[side], offset))

    alphas, betas = {}, {}
    for offset in (2, 1, 3, 0):
        alphas[offset] = send(0, offset)
        betas[offset] = send(1, offset)
    lefts, rights = [], []
    image = jnp.zeros((OWNED, B, B), F32)
    for offset in (2, 1, 3, 0):
        left, right, image = arrive(block_sizes, psi_guess, image, alphas[offset], betas[offset])
        lefts.append(left)
        rights.append(right)
    volume = float(psi_guess.shape[1] * B * B)
    basis, report = krylov(block_sizes, psi_guess, lefts, rights, image)
    report = lax.psum(report, "term")
    vector, energy = davidson(report, basis, volume)
    return vector, energy


def solution(mesh):
    segments, groups = mesh.shape["chain"], mesh.shape["term"]
    placed = (
        P("chain", None, None, None),
        P("chain", None, None, None),
        P("chain", "term", None, None, None),
        P("chain", "term", None, None, None),
        P("chain", None, None),
    )
    return jax.shard_map(
        functools.partial(local, segments, groups),
        mesh=mesh,
        in_specs=placed,
        out_specs=(P("chain", "term", None, None), P("chain")),
        check_vma=False,
    )
```

```python
import functools
import math

import jax
import jax.numpy as jnp
from jax import lax
from jax.experimental import pallas as pl
from jax.experimental.pallas import tpu as pltpu
from jax.sharding import PartitionSpec as P

ITERS = 4
NVEC = ITERS + 2
twist_scale = 0.22
shrink = 1.047
epsilon = 1e-06

B = 128
HALF = 64
F32 = jnp.float32
BF16 = jnp.bfloat16

OWNED = 2
LOCAL_TERMS = 8
MATS = OWNED * LOCAL_TERMS
DIAG_ROW = MATS * HALF
MSG_ROWS = DIAG_ROW + MATS // 2


def split(value):
    high = value.astype(BF16)
    low = (value - high.astype(F32)).astype(BF16)
    return high, low


def dot(left, right):
    return jnp.dot(left, right, preferred_element_type=F32)


def iotas(rows):
    row = lax.broadcasted_iota(jnp.int32, (rows, B), 0)
    lane = lax.broadcasted_iota(jnp.int32, (rows, B), 1)
    return row, lane


def swap_halves(value):
    return pltpu.roll(value, HALF, 1)


def dress_kernel(segments, groups, jobs, left_hbm, right_hbm, raw_hbm, *refs):
    outs, (env_ref, raw_ref, env_sem, raw_sem) = refs[: len(jobs)], refs[len(jobs) :]
    seg = lax.axis_index("chain")
    odd = lax.rem(seg, 2) == 1
    edge = jnp.logical_or(seg == 0, seg == segments - 1)

    def first_sector(slot):
        return OWNED * lax.rem(lax.axis_index("term") + jobs[slot][1], groups)

    def env_copy(source, slot, owned):
        part = source.at[0, :, first_sector(slot) + owned]
        return pltpu.make_async_copy(part, env_ref.at[slot, owned], env_sem.at[slot, owned])

    def raw_copy(slot):
        part = raw_hbm.at[0, pl.ds(first_sector(slot), OWNED)]
        return pltpu.make_async_copy(part, raw_ref.at[slot], raw_sem.at[slot])

    for slot, (side, _) in enumerate(jobs):
        raw_copy(slot).start()
        take_left = jnp.logical_not(odd) if side else jnp.logical_xor(odd, edge)

        @pl.when(take_left)
        def _():
            for owned in range(OWNED):
                env_copy(left_hbm, slot, owned).start()

        @pl.when(jnp.logical_not(take_left))
        def _():
            for owned in range(OWNED):
                env_copy(right_hbm, slot, owned).start()

    row, lane = iotas(B)
    eye = jnp.where(row == lane, 1.0, 0.0).astype(F32)
    sign = jnp.where(odd, 1.0, -1.0).astype(F32)
    row_h, lane_h = iotas(HALF)
    keep_top = jnp.logical_or(lane_h >= HALF, lane_h >= row_h)
    on_diag_high = lane_h - HALF == row_h
    on_diag_low = lane_h == row_h
    pairs = LOCAL_TERMS // 2
    for slot, (side, _) in enumerate(jobs):
        raw_copy(slot).wait()
        out_ref = outs[slot]
        if side:
            even, coef = eye * (1.0 / shrink), -sign
        else:
            even = eye * jnp.where(edge, 1.0, 1.0 / shrink).astype(F32)
            coef = jnp.where(edge, 0.0, sign).astype(F32)
        coef = coef * (twist_scale / math.sqrt(2.0 * B) / shrink)
        factors = []
        for owned in range(OWNED):
            raw = raw_ref[slot, owned]
            odd_part = (raw - raw.T) * coef
            high, low = split((even + odd_part) * 0.5)
            right_op = jnp.concatenate([jnp.concatenate([high, low], 1)] * 2, 0)
            high, low = split(even - odd_part)
            left_op = jnp.concatenate([jnp.concatenate([high] * 2, 1), jnp.concatenate([low] * 2, 1)], 0)
            factors.append((left_op, right_op))
        for owned in range(OWNED):
            env_copy(left_hbm, slot, owned).wait()
        work = [(owned, pair) for owned in range(OWNED) for pair in range(pairs)]
        parts = []
        for owned, pair in work:
            sums = []
            for term in (2 * pair, 2 * pair + 1):
                env = env_ref[slot, owned, term]
                high, low = split(env + env.T)
                sums.append(jnp.concatenate([high, low], 1))
            parts.append(dot(jnp.concatenate(sums, 0), factors[owned][1]))
        fulls = []
        for (owned, pair), part in zip(work, parts):
            high, low = split(part[:, :B] + part[:, B:])
            right_side = jnp.concatenate(
                [jnp.concatenate([high[:B], high[B:]], 1), jnp.concatenate([low[:B], low[B:]], 1)], 0
            )
            full = dot(factors[owned][0], right_side)
            fulls.append(full[:B] + full[B:])
        for index, full in enumerate(fulls):
            diag = jnp.zeros((HALF, B), F32)
            for j in range(2):
                mat = full[:, j * B : (j + 1) * B]
                top, bottom = mat[:HALF], mat[HALF:]
                turned = swap_halves(bottom)
                start = (2 * index + j) * HALF
                out_ref[start : start + HALF, :] = jnp.where(keep_top, top, turned)
                if j == 0:
                    diag = jnp.where(on_diag_high, bottom, diag)
                else:
                    diag = jnp.where(on_diag_low, turned, diag)
            start = DIAG_ROW + index
            out_ref[start : start + 1, :] = jnp.sum(diag, axis=0, keepdims=True)


TINY = pl.CostEstimate(flops=1000, bytes_accessed=1000, transcendentals=0)
VMEM = pl.BlockSpec(memory_space=pltpu.VMEM)
SMEM = pl.BlockSpec(memory_space=pltpu.SMEM)
BLOCK_ROWS = MATS * B


def dress(left_env, right_env, raw, jobs, segments, groups, limit):
    count = len(jobs)
    return pl.pallas_call(
        functools.partial(dress_kernel, segments, groups, jobs),
        out_shape=(jax.ShapeDtypeStruct((MSG_ROWS, B), F32),) * count,
        in_specs=[pl.BlockSpec(memory_space=pltpu.HBM)] * 3,
        out_specs=(VMEM,) * count,
        scratch_shapes=[
            pltpu.VMEM((count, OWNED, LOCAL_TERMS, B, B), F32),
            pltpu.VMEM((count, OWNED, B, B), F32),
            pltpu.SemaphoreType.DMA((count, OWNED)),
            pltpu.SemaphoreType.DMA((count,)),
        ],
        compiler_params=pltpu.CompilerParams(vmem_limit_bytes=limit << 20),
        cost_estimate=TINY,
        name="dress",
    )(left_env, right_env, raw)


def total(value):
    tiles = jnp.sum(value.reshape(OWNED * B // 8, 8, B), axis=0)
    return jnp.sum(jnp.sum(tiles, axis=0, keepdims=True), axis=1, keepdims=True)


def unpack(msg_ref, pairs):
    row_h, lane_h = iotas(HALF)
    keep_top = jnp.logical_or(lane_h >= HALF, lane_h >= row_h)
    keep_bottom = jnp.logical_and(lane_h >= HALF, lane_h - HALF < row_h)
    on_diag = lane_h - HALF == row_h
    packed = [msg_ref[2 * pair * HALF : (2 * pair + 2) * HALF, :] for pair in pairs]
    diags = [msg_ref[DIAG_ROW + pair : DIAG_ROW + pair + 1, :] for pair in pairs]
    out = []
    for pair_value, diag_row in zip(packed, diags):
        for j in range(2):
            value = pair_value[j * HALF : (j + 1) * HALF]
            turned = swap_halves(value)
            flipped = jnp.concatenate([value, turned], 0).T
            diag = diag_row if j == 0 else swap_halves(diag_row)
            top = jnp.where(keep_top, value, flipped[:HALF])
            bottom = jnp.where(keep_bottom, turned, flipped[HALF:])
            bottom = jnp.where(on_diag, jnp.broadcast_to(diag, (HALF, B)), bottom)
            high, low = split(jnp.concatenate([top, bottom], 0))
            out.append(jnp.concatenate([high, low], 1))
    return out


def doubled(vector):
    high, low = split(vector)
    return jnp.concatenate([jnp.concatenate([high, low], 1)] * 2, 0)


def between(half):
    high, low = split(half[:, :B] + half[:, B:])
    return jnp.concatenate(
        [jnp.concatenate([high[:B], high[B:]], 1), jnp.concatenate([low[:B], low[B:]], 1)], 0
    )


def quarters(out):
    return (out[:B, :B] + out[:B, B:]) + (out[B:, :B] + out[B:, B:])


def live_mask(sizes_ref, owned):
    odd = lax.rem(lax.axis_index("chain"), 2) == 1
    sector = OWNED * lax.axis_index("term") + owned
    row, lane = iotas(B)
    rows_live = sizes_ref[0, 0, sector]
    cols_live = sizes_ref[0, 1, sector]
    first = jnp.where(odd, cols_live, rows_live)
    second = jnp.where(odd, rows_live, cols_live)
    return jnp.where(jnp.logical_and(row < first, lane < second), 1.0, 0.0).astype(F32)


def start_vector(sizes_ref, psi_ref, owned):
    odd = lax.rem(lax.axis_index("chain"), 2) == 1
    guess = psi_ref[0, OWNED * lax.axis_index("term") + owned]
    return jnp.where(odd, guess.T, guess) * live_mask(sizes_ref, owned)


def open_blocks(sizes_ref, psi_ref, message_ref, blocks_ref, mids_ref):
    pairs = LOCAL_TERMS // 2
    for owned in range(OWNED):
        vector = doubled(start_vector(sizes_ref, psi_ref, owned))
        blocks = unpack(message_ref, [owned * pairs + i for i in range(pairs)])
        for i in range(pairs):
            both = jnp.concatenate(blocks[2 * i : 2 * i + 2], 0)
            start = (owned * pairs + i) * 2 * B
            blocks_ref[start : start + 2 * B, :] = both
            mids_ref[owned, :, 2 * i * B : 2 * (i + 1) * B] = between(dot(both, vector))


def apply_blocks(mids_ref, message_ref, blocks_ref):
    pairs = LOCAL_TERMS // 2
    out = []
    for owned in range(OWNED):
        blocks = jnp.concatenate(unpack(message_ref, [owned * pairs + i for i in range(pairs)]), 0)
        start = owned * LOCAL_TERMS * B
        blocks_ref[start : start + LOCAL_TERMS * B, :] = blocks
        out.append(quarters(dot(mids_ref[owned], blocks)))
    return jnp.stack(out, 0)


def begin_kernel(sizes_ref, psi_ref, alpha_ref, beta_ref, next_ref, left_ref, right_ref, next_left_ref, mids_ref, image_ref, own_ref):
    open_blocks(sizes_ref, psi_ref, alpha_ref, left_ref, own_ref)
    image_ref[...] = apply_blocks(own_ref, beta_ref, right_ref)
    open_blocks(sizes_ref, psi_ref, next_ref, next_left_ref, mids_ref)


def open_kernel(sizes_ref, psi_ref, _, one_ref, two_ref, left_one_ref, left_two_ref, mids_one_ref, mids_two_ref):
    open_blocks(sizes_ref, psi_ref, one_ref, left_one_ref, mids_one_ref)
    open_blocks(sizes_ref, psi_ref, two_ref, left_two_ref, mids_two_ref)


def close_kernel(*refs):
    before_ref, mids, messages, rights, image_ref = refs[0], refs[1:4], refs[4:7], refs[7:10], refs[10]
    image = before_ref[...]
    for i in range(3):
        image = image + apply_blocks(mids[i], messages[i], rights[i])
    image_ref[...] = image


BLOCKS = jax.ShapeDtypeStruct((BLOCK_ROWS, 2 * B), BF16)
MIDS = jax.ShapeDtypeStruct((OWNED, 2 * B, LOCAL_TERMS * B), BF16)
IMAGE = jax.ShapeDtypeStruct((OWNED, B, B), F32)


def call(kernel, out_shape, name, *operands, scalars=0, scratch=()):
    return pl.pallas_call(
        kernel,
        out_shape=out_shape,
        in_specs=[SMEM] * scalars + [VMEM] * (len(operands) - scalars),
        out_specs=(VMEM,) * len(out_shape),
        scratch_shapes=scratch,
        compiler_params=pltpu.CompilerParams(vmem_limit_bytes=16 << 20),
        cost_estimate=TINY,
        name=name,
    )(*operands)


def krylov_kernel(sizes_ref, psi_ref, *refs):
    lefts, rights, image_ref = refs[0:4], refs[4:8], refs[8]
    basis_ref, report_ref = refs[9:11]
    vec_ref, acc_ref, mask_ref = refs[11:]
    group = lax.axis_index("term")
    starts = []
    for owned in range(OWNED):
        mask_ref[owned] = live_mask(sizes_ref, owned)
        starts.append(start_vector(sizes_ref, psi_ref, owned))
    vector = jnp.stack(starts, 0)

    def apply_ham():
        acc_ref[...] = jnp.zeros_like(acc_ref)

        def body(index, carry):
            units = []
            for owned in range(OWNED):
                start = pl.multiple_of((owned * (LOCAL_TERMS // 2) + index) * 2 * B, 2 * B)
                units.append([between(dot(left[pl.ds(start, 2 * B), :], vec_ref[owned])) for left in lefts])
            for owned in range(OWNED):
                start = pl.multiple_of((owned * (LOCAL_TERMS // 2) + index) * 2 * B, 2 * B)
                right = jnp.concatenate([ref[pl.ds(start, 2 * B), :] for ref in rights], 0)
                acc_ref[owned] += quarters(dot(jnp.concatenate(units[owned], 1), right))
            return carry

        lax.fori_loop(0, LOCAL_TERMS // 2, body, 0, unroll=True)
        return acc_ref[...] * mask_ref[...]

    def inverse_norm(square):
        return jnp.where(square > 0.0, lax.rsqrt(jnp.where(square > 0.0, square, 1.0)), 0.0)

    lane_1 = lax.broadcasted_iota(jnp.int32, (1, B), 1)
    report = jnp.zeros((1, B), F32)

    def put(report, slot, value):
        return jnp.where(lane_1 == slot, value, report)

    grams = []

    def partial_dot(first, second):
        return jnp.sum((first * second).reshape(OWNED * B, B), axis=0, keepdims=True)

    square = total(vector * vector)
    scale = inverse_norm(square)
    report = put(report, 0, square * scale)
    basis_ref[0] = vector * scale
    previous_beta = None
    for step in range(NVEC - 1):
        current = basis_ref[step]
        if step:
            for owned in range(OWNED):
                vec_ref[owned] = doubled(current[owned])
            image = apply_ham()
        else:
            image = image_ref[...] * mask_ref[...] * scale
        alpha = total(current * image)
        rest = image - alpha * current
        if step:
            rest = rest - previous_beta * basis_ref[step - 1]
        square = total(rest * rest)
        scale = inverse_norm(square)
        beta = square * scale
        basis_ref[step + 1] = rest * scale
        grams += [partial_dot(basis_ref[step], basis_ref[i]) for i in range(step + 1)]
        report = put(report, 1 + step, alpha)
        report = put(report, 1 + (NVEC - 1) + step, beta)
        previous_beta = beta
    grams += [partial_dot(basis_ref[NVEC - 1], basis_ref[i]) for i in range(NVEC)]
    first = 1 + 2 * (NVEC - 1)
    rows = [jnp.zeros((1, B), F32)] * first + grams
    rows += [jnp.zeros((1, B), F32)] * (B - len(rows))
    summed = jnp.sum(jnp.concatenate(rows, 0).T, axis=0, keepdims=True)
    report = report + summed
    row_8, _ = iotas(8)
    report_ref[...] = jnp.where(row_8 == group, jnp.broadcast_to(report, (8, B)), 0.0)


def krylov(sizes, psi, lefts, rights, image):
    return pl.pallas_call(
        krylov_kernel,
        out_shape=(
            jax.ShapeDtypeStruct((NVEC, OWNED, B, B), F32),
            jax.ShapeDtypeStruct((8, B), F32),
        ),
        in_specs=[SMEM] + [VMEM] * 10,
        out_specs=(VMEM, VMEM),
        scratch_shapes=[
            pltpu.VMEM((OWNED, 2 * B, 2 * B), BF16),
            pltpu.VMEM((OWNED, B, B), F32),
            pltpu.VMEM((OWNED, B, B), F32),
        ],
        compiler_params=pltpu.CompilerParams(vmem_limit_bytes=24 << 20),
        cost_estimate=TINY,
        name="krylov",
    )(sizes, psi, *lefts, *rights, image)


def davidson_kernel(volume, *refs):
    *reports, basis_ref, out_ref, energy_ref = refs
    odd = lax.rem(lax.axis_index("chain"), 2) == 1
    group = lax.axis_index("term")
    report = functools.reduce(jnp.add, [ref[...] for ref in reports])
    row_8, lane_8 = iotas(8)

    def column(slot):
        return jnp.sum(jnp.where(lane_8 == slot, report, 0.0), axis=1, keepdims=True)

    weight = column(0)
    alphas = [column(1 + i) for i in range(NVEC - 1)]
    betas = [column(NVEC + i) for i in range(NVEC - 1)]
    gram = {}
    slot = 1 + 2 * (NVEC - 1)
    for j in range(NVEC):
        for i in range(j + 1):
            gram[i, j] = gram[j, i] = column(slot)
            slot += 1

    def mean_dot(first, second):
        parts = None
        for i, a in enumerate(first):
            inner = None
            for j, b in enumerate(second):
                piece = gram[i, j] * b
                inner = piece if inner is None else inner + piece
            piece = a * inner
            parts = piece if parts is None else parts + piece
        return jnp.sum(parts, axis=0, keepdims=True) / volume

    def apply_ham(vector):
        size = len(vector)
        out = []
        for i in range(size + 1):
            value = jnp.zeros((8, 1), F32)
            if i < size:
                value = value + alphas[i] * vector[i]
            if i >= 1:
                value = value + betas[i - 1] * vector[i - 1]
            if i + 1 < size:
                value = value + betas[i] * vector[i + 1]
            out.append(value)
        return out

    def combine(a, first, b, second):
        out = []
        for i in range(max(len(first), len(second))):
            value = None
            if i < len(first):
                value = a * first[i]
            if i < len(second):
                piece = b * second[i]
                value = piece if value is None else value + piece
            out.append(value)
        return out

    started = [weight]
    norm = jnp.sqrt(mean_dot(started, started) + epsilon)
    vector = [weight / norm]
    image = apply_ham(vector)
    energy = mean_dot(vector, image)
    for _ in range(ITERS):
        residual = combine(1.0, image, -energy, vector)
        norm = jnp.sqrt(mean_dot(residual, residual) + epsilon)
        along = mean_dot(residual, image) / norm
        unit = [value / norm for value in residual]
        image_unit = apply_ham(unit)
        curve = mean_dot(unit, image_unit)
        gap_half = 0.5 * (curve - energy)
        lowest = 0.5 * (curve + energy) - jnp.sqrt(gap_half * gap_half + along * along)
        coef_b = lowest - energy
        combined = jnp.sqrt(along * along + coef_b * coef_b)
        vector = combine(along / combined, vector, coef_b / combined, unit)
        image = combine(along / combined, image, coef_b / combined, image_unit)
        energy = lowest

    mine = lax.broadcasted_iota(jnp.int32, (8, 1), 0) == group
    coefs = [jnp.sum(jnp.where(mine, value, 0.0), axis=0, keepdims=True) for value in vector]
    for owned in range(OWNED):
        value = None
        for i, coef in enumerate(coefs):
            piece = coef * basis_ref[i, owned]
            value = piece if value is None else value + piece
        out_ref[0, owned] = jnp.where(odd, value.T, value)
    energy_ref[0] = energy[0, 0]


def davidson(reports, basis, volume):
    return pl.pallas_call(
        functools.partial(davidson_kernel, volume),
        out_shape=(
            jax.ShapeDtypeStruct((1, OWNED, B, B), F32),
            jax.ShapeDtypeStruct((1,), F32),
        ),
        in_specs=[VMEM] * (len(reports) + 1),
        out_specs=(VMEM, SMEM),
        compiler_params=pltpu.CompilerParams(vmem_limit_bytes=16 << 20),
        cost_estimate=TINY,
        name="davidson",
    )(*reports, basis)


ORDER = (
    (((1, 2),), 20),
    (((0, 2), (0, 1)), 20),
    (((1, 1), (0, 3)), 20),
    (((1, 3), (0, 0)), 20),
    (((1, 0),), 20),
)


def exchange_pairs(segments, groups, partner, offset):
    return [
        (seg * groups + term, partner(seg) * groups + (term + offset) % groups)
        for seg in range(segments)
        for term in range(groups)
    ]


def local(segments, groups, psi_guess, transfer_raw, left_env, right_env, block_sizes):
    def alpha_partner(seg):
        if seg in (0, segments - 1):
            return seg
        return seg + 1 if seg % 2 else seg - 1

    def beta_partner(seg):
        return seg ^ 1

    partners = (alpha_partner, beta_partner)
    left_env, right_env, raw = [
        pltpu.with_memory_space_constraint(value, pltpu.HBM) for value in (left_env, right_env, transfer_raw)
    ]
    messages = {}
    for jobs, limit in ORDER:
        made = dress(left_env, right_env, raw, jobs, segments, groups, limit)
        made, raw = lax.optimization_barrier((made, raw))
        for job, message in zip(jobs, made):
            messages[job] = message

    def send(side, offset, after=None):
        message = messages[side, offset]
        if after is not None:
            message, _ = lax.optimization_barrier((message, after))
        return lax.ppermute(message, ("chain", "term"), exchange_pairs(segments, groups, partners[side], offset))

    alphas, betas = {}, {}
    for offset in (2, 1, 3):
        alphas[offset] = send(0, offset)
        betas[offset] = send(1, offset)
    alphas[0] = send(0, 0, betas[2])
    betas[0] = send(1, 0, alphas[1])
    lefts, rights = {}, {}
    lefts[2], rights[2], lefts[1], mids_1, image = call(
        begin_kernel, (BLOCKS, BLOCKS, BLOCKS, MIDS, IMAGE), "begin",
        block_sizes, psi_guess, alphas[2], betas[2], alphas[1],
        scalars=1, scratch=[pltpu.VMEM(MIDS.shape, BF16)],
    )
    lefts[3], lefts[0], mids_3, mids_0 = call(
        open_kernel, (BLOCKS, BLOCKS, MIDS, MIDS), "open", block_sizes, psi_guess, image, alphas[3], alphas[0], scalars=1
    )
    rights[1], rights[3], rights[0], image = call(
        close_kernel, (BLOCKS, BLOCKS, BLOCKS, IMAGE), "close",
        image, mids_1, mids_3, mids_0, betas[1], betas[3], betas[0],
    )
    lefts, rights = [[side[offset] for offset in range(groups)] for side in (lefts, rights)]
    volume = float(psi_guess.shape[1] * B * B)
    basis, report = krylov(block_sizes, psi_guess, lefts, rights, image)
    reports = [report]
    for shift in range(1, groups):
        turn = [(term, (term + shift) % groups) for term in range(groups)]
        reports.append(lax.ppermute(report, "term", turn))
    vector, energy = davidson(reports, basis, volume)
    return vector, energy


def solution(mesh):
    segments, groups = mesh.shape["chain"], mesh.shape["term"]
    placed = (
        P("chain", None, None, None),
        P("chain", None, None, None),
        P("chain", "term", None, None, None),
        P("chain", "term", None, None, None),
        P("chain", None, None),
    )
    return jax.shard_map(
        functools.partial(local, segments, groups),
        mesh=mesh,
        in_specs=placed,
        out_specs=(P("chain", "term", None, None), P("chain")),
        check_vma=False,
    )
```
